256 devices in a mesh: section: 2 (over core), ctx: 128 (over y, z, x).
Axes of the slice: x: 4, y: 4, z: 8, core: 2. Of those that a mesh axis runs over, the one named last changes fastest.
Arguments:
- queries: bfloat16 [2, 8192, 4096], P('section', 'ctx'), may hold values from -80 to 80
- key_rows: bfloat16 [2, 8192, 512], P('section', 'ctx'), may hold values from -8 to 8
- rows_of_value: bfloat16 [2, 8192, 512], P('section', 'ctx'), may hold values from -6 to 6
- query_gain: float32 [4096], replicated, may hold values from 2 to 6
- block_order: int32 [256], replicated, may hold values from 0 to 255, each once
Outputs:
- attended: bfloat16 [2, 8192, 4096], P('section', 'ctx')
The draws below stay inside these ranges and needn't reach their ends.
Inputs may be any that keep to these rules, and one draw needn't show every extreme that they name: A permutation; stored block j of 32 rows holds the sequence's block block_order[j].
All inputs are finite; a program needn't handle non-finite values.
Results may differ from the reference program's by a relative error of at most 0.0085.
Values may be sent and summed in bfloat16 or wider, within the bound.
A program may use at most 192 MiB of HBM per device.

```python
import math
import jax
import jax.numpy as jnp
from jax import lax

HQ = 32
KEY_VALUE_HEADS = 4
HEAD_SIZE = 128
QUERY_PER_GROUP = 8
BLK = 32
BLOCKS = 256
TOKEN_COUNT = 8192
LAYER_TOTAL = 2


def drawn_pair(key):
    base = jax.random.fold_in(key, 4242)
    key_query, random_key = jax.random.split(base, 2)
    query_base = jnp.clip(1.5 * jax.random.normal(key_query, (LAYER_TOTAL, TOKEN_COUNT, HQ * HEAD_SIZE), jnp.float32), -8.0, 8.0)
    key_offset = jnp.clip(1.5 * jax.random.normal(random_key, (LAYER_TOTAL, TOKEN_COUNT, KEY_VALUE_HEADS * HEAD_SIZE), jnp.float32), -8.0, 8.0)
    return (query_base, key_offset)


def draw_queries(key, part):
    return drawn_pair(key)[0].astype(jnp.bfloat16)


def draw_key_rows(key, part):
    return drawn_pair(key)[1].astype(jnp.bfloat16)


def block_scale(key, dims, shards, least, largest):
    loudness, own = 1.0, jax.random.fold_in(key, 6)
    for dim, blocks in shards:
        draws = jnp.exp(jax.random.uniform(jax.random.fold_in(own, dim), (blocks,), jnp.float32, least / len(shards), largest / len(shards)))
        loudness = loudness * jnp.repeat(draws, dims[dim] // blocks).reshape([-1 if axis == dim else 1 for axis in range(len(dims))])
    return loudness


def noise(rng, extent, scale, bound, cuts=(), kind=jnp.bfloat16):
    values = scale * jax.random.normal(rng, extent, jnp.float32)
    if cuts:
        values = values * block_scale(rng, extent, cuts, -0.22, 0.18)
    return jnp.clip(values, -bound, bound).astype(kind)


def setup_inputs(seed: int = 0) -> dict:
    seeds = jax.random.split(jax.random.key(seed), 6)
    queries = draw_queries(jax.random.fold_in(seeds[5], 71), 0)
    key_rows = draw_key_rows(jax.random.fold_in(seeds[5], 71), 0)
    rows_of_value = noise(seeds[2], (LAYER_TOTAL, TOKEN_COUNT, KEY_VALUE_HEADS * HEAD_SIZE), 1.0, 6.0, ((0, 2), (1, 128)))
    query_gain = jnp.clip(jnp.exp(jax.random.uniform(seeds[3], (HQ * HEAD_SIZE,), jnp.float32, math.log(2.0), math.log(6.0))), 2.0, 6.0)
    block_order = jax.random.permutation(seeds[4], BLOCKS).astype(jnp.int32)
    return dict(queries=queries, key_rows=key_rows, rows_of_value=rows_of_value, query_gain=query_gain, block_order=block_order)


def slot_positions(block_order):
    row_ids = jnp.arange(TOKEN_COUNT, dtype=jnp.int32)
    return block_order[row_ids // BLK] * BLK + row_ids % BLK

def attend(rows_of_query, key_portion, value_portion, positions):
    width_of_block = math.gcd(TOKEN_COUNT, 256)
    key_matrix_full = key_portion.astype(jnp.float32).reshape(TOKEN_COUNT, KEY_VALUE_HEADS, HEAD_SIZE)
    value_matrix_full = value_portion.astype(jnp.float32).reshape(TOKEN_COUNT, KEY_VALUE_HEADS, HEAD_SIZE)
    score_scale = 1.0 / math.sqrt(HEAD_SIZE)

    def one_block(block_index):
        first_row_index = (block_index * width_of_block).astype(jnp.int32)
        block_of_query = lax.dynamic_slice_in_dim(rows_of_query, first_row_index, width_of_block, 0).reshape(width_of_block, KEY_VALUE_HEADS, QUERY_PER_GROUP, HEAD_SIZE)
        query_pos = lax.dynamic_slice_in_dim(positions, first_row_index, width_of_block, 0)
        scores = jnp.einsum('qjgd,kjd->jgqk', block_of_query, key_matrix_full, precision=lax.Precision.HIGHEST) * score_scale
        visible = positions[None, :] <= query_pos[:, None]
        scores = jnp.where(visible, scores, -jnp.inf)
        row_max = lax.optimization_barrier(jnp.max(scores, axis=-1, keepdims=True))
        weights = jnp.exp(scores - row_max)
        row_sum = lax.optimization_barrier(jnp.sum(weights, axis=-1))
        rounded = weights.astype(jnp.bfloat16)
        rounded = lax.optimization_barrier(rounded).astype(jnp.float32)
        mixed_out = jnp.einsum('jgqk,kjd->qjgd', rounded, value_matrix_full, precision=lax.Precision.HIGHEST)
        mixed_out = mixed_out / jnp.transpose(row_sum, (2, 0, 1))[..., None]
        return mixed_out.reshape(width_of_block, HQ * HEAD_SIZE)
    blocks_out = lax.map(one_block, jnp.arange(TOKEN_COUNT // width_of_block, dtype=jnp.int32))
    return blocks_out.reshape(TOKEN_COUNT, HQ * HEAD_SIZE)

def reference(queries, key_rows, rows_of_value, query_gain, block_order):
    positions = slot_positions(block_order)
    first_out = attend(queries[0].astype(jnp.float32), key_rows[0], rows_of_value[0], positions).astype(jnp.bfloat16)
    shifted = (queries[1].astype(jnp.float32) + query_gain[None, :] * first_out.astype(jnp.float32)).astype(jnp.bfloat16)
    shifted = lax.optimization_barrier(shifted).astype(jnp.float32)
    second = attend(shifted, key_rows[1], rows_of_value[1], positions).astype(jnp.bfloat16)
    return jnp.stack([first_out, second])
```

```python
import math

import jax
import jax.numpy as jnp
from jax import lax
from jax.experimental import pallas as pl
from jax.experimental.pallas import tpu as pltpu
from jax.sharding import PartitionSpec as P

MESH = pl.DeviceIdType.MESH
HEAD = 128
NX, NY, NZ = 4, 4, 8
GROUPS = NY * NZ
LOG2_SCALE = math.log2(math.e) / math.sqrt(HEAD)
MASKED = -1e30
KEY_TILE = 512
ROW_TILE = 256


def ring_events(na, nb):
    def offsets(n):
        return [0] + [s * d for d in range(1, n // 2) for s in (1, -1)] + [n // 2]

    events = [(a, b) for a in offsets(na) for b in offsets(nb)]
    return sorted(events, key=lambda e: (abs(e[0]) + abs(e[1]), abs(e[1])))


def here():
    section = lax.axis_index("section")
    ctx = lax.axis_index("ctx")
    return section, ctx, ctx // NX, ctx % NX


def greet(partners):
    barrier = pltpu.get_barrier_semaphore()
    for device in partners:
        pl.semaphore_signal(barrier, inc=1, device_id=device, device_id_type=MESH)
    pl.semaphore_wait(barrier, len(partners))


def remote(src, dst, send_sem, recv_sem, device):
    return pltpu.make_async_remote_copy(
        src_ref=src, dst_ref=dst, send_sem=send_sem, recv_sem=recv_sem,
        device_id=device, device_id_type=MESH,
    )


def group_partner(section, group, x, step):
    other = lax.rem(section * NX + x + step, 2 * NX)
    return other // NX, other % NX, (other // NX, group * NX + other % NX)


def gather_kernel(q_ref, k_ref, v_ref, qx_ref, kv_ref, q_send, q_recv, x_send, x_recv,
                  ring_send, ring_recv, sib_send, sib_recv, own_sem):
    section, ctx, group, x = here()
    y, z = group // NZ, group % NZ

    def at(y_at, z_at):
        return (section, (lax.rem(y_at + NY, NY) * NZ + lax.rem(z_at + NZ, NZ)) * NX + x)

    partners = [group_partner(section, group, x, step)[2] for step in range(1, 2 * NX)]
    greet(partners + [at(y + 1, z), at(y - 1, z), at(y, z + 1), at(y, z - 1)])

    exchanged = []
    for step in range(1, NX):
        x_to = lax.rem(x + step, NX)
        columns = pl.ds(pl.multiple_of(x_to * HEAD, HEAD), HEAD)
        for which, ref in ((0, k_ref), (1, v_ref)):
            copy = remote(
                ref.at[0, :, columns], kv_ref.at[section, group, x, which],
                x_send.at[step - 1, which], x_recv.at[step - 1, which],
                (section, group * NX + x_to),
            )
            copy.start()
            exchanged.append(copy)
    own = []
    columns = pl.ds(pl.multiple_of(x * HEAD, HEAD), HEAD)
    for which, ref in ((0, k_ref), (1, v_ref)):
        own.append(pltpu.make_async_copy(
            ref.at[0, :, columns], kv_ref.at[section, group, x, which], own_sem.at[which]))
    own.append(pltpu.make_async_copy(
        q_ref.at[0, :, pl.ds(pl.multiple_of(x * 1024 + section * 512, 512), 512)],
        qx_ref.at[section, x], own_sem.at[2]))
    for copy in own:
        copy.start()
    moved = []
    for step in range(1, 2 * NX):
        core_to, x_to, device = group_partner(section, group, x, step)
        copy = remote(
            q_ref.at[0, :, pl.ds(pl.multiple_of(x_to * 1024 + core_to * 512, 512), 512)],
            qx_ref.at[section, x], q_send.at[step - 1], q_recv.at[step - 1], device,
        )
        copy.start()
        moved.append(copy)
    for copy in own:
        copy.wait()
    for copy in exchanged:
        copy.wait_recv()

    def rings(na, nb, z_first):
        index = {e: i for i, e in enumerate(ring_events(na, nb))}
        sends = []

        def chunk(a, b):
            y_from, z_from = (y - b, z - a) if z_first else (y - a, z - b)
            return lax.rem(y_from + NY, NY) * NZ + lax.rem(z_from + NZ, NZ)

        def neighbour(da, db):
            return at(y + db, z + da) if z_first else at(y + da, z + db)

        def part(g, half):
            if half is None:
                return kv_ref.at[section, g]
            return kv_ref.at[section, g, pl.ds(2 * half, 2)]

        def copies(g, event, half, device):
            slot = (index[event], 1 if half == 1 else 0)
            piece = part(g, half)
            return remote(piece, piece, ring_send.at[slot], ring_recv.at[slot], device)

        def send(g, event, half, da, db):
            copy = copies(g, event, half, neighbour(da, db))
            copy.start()
            sends.append(copy)

        def halves(d, n):
            return d == n // 2

        siblings = []
        for event, i in index.items():
            a, b = event
            g = chunk(a, b)
            if event != (0, 0):
                if (b != 0 and halves(b, nb)) or (b == 0 and halves(a, na)):
                    for half in (0, 1):
                        copies(g, event, half, at(y, z + 1)).wait_recv()
                else:
                    copies(g, event, None, at(y, z + 1)).wait_recv()
            if b == 0 and not halves(a, na):
                for sign in (1, -1):
                    if a * sign < 0:
                        continue
                    to = a + sign
                    if abs(to) == na // 2:
                        send(g, (na // 2, 0), 0 if sign > 0 else 1, sign, 0)
                    else:
                        send(g, (to, 0), None, sign, 0)
            if not (b != 0 and halves(b, nb)):
                for sign in (1, -1):
                    if b * sign < 0:
                        continue
                    to = b + sign
                    if abs(to) == nb // 2:
                        send(g, (a, nb // 2), 0 if sign > 0 else 1, 0, sign)
                    else:
                        send(g, (a, to), None, 0, sign)
            copy = remote(kv_ref.at[section, g], kv_ref.at[section, g], sib_send.at[i],
                          sib_recv.at[i], (1 - section, ctx))
            copy.start()
            siblings.append(copy)
        for copy in siblings:
            copy.wait_recv()
        for copy in sends + siblings:
            copy.wait_send()

    @pl.when(section == 0)
    def _():
        rings(NZ, NY, True)

    @pl.when(section == 1)
    def _():
        rings(NY, NZ, False)

    for copy in moved:
        copy.wait()
    for copy in exchanged:
        copy.wait_send()


def gather(queries, keys, values):
    rows = queries.shape[1]
    dma = pltpu.SemaphoreType.DMA
    any_spec = pl.BlockSpec(memory_space=pl.ANY)
    return pl.pallas_call(
        gather_kernel,
        out_shape=(
            jax.ShapeDtypeStruct((2, NX, rows, 4 * HEAD), jnp.bfloat16),
            jax.ShapeDtypeStruct((2, GROUPS, NX, 2, rows, HEAD), jnp.bfloat16),
        ),
        in_specs=[any_spec] * 3,
        out_specs=(any_spec, any_spec),
        scratch_shapes=[
            dma((7,)), dma((7,)), dma((3, 2)), dma((3, 2)), dma((32, 2)), dma((32, 2)),
            dma((32,)), dma((32,)), dma((3,)),
        ],
        compiler_params=pltpu.CompilerParams(collective_id=0, has_side_effects=True),
    )(queries, keys, values)


def attend_kernel(qx_ref, kv_hbm, bias_ref, hot_ref, gain_ref, o_ref, kv_ref, qa, m_s, acc_s, sem):
    group = lax.axis_index("ctx") // NX
    loads = [pltpu.make_async_copy(kv_hbm.at[l], kv_ref.at[l], sem.at[l]) for l in range(2)]
    for copy in loads:
        copy.start()

    def widen(v):
        return jnp.concatenate([v, jnp.ones(v.shape, jnp.bfloat16)], axis=1)

    def product(q, k):
        return lax.dot_general(q, k, (((1,), (1,)), ((), ())), preferred_element_type=jnp.float32)

    for layer in range(2):
        loads[layer].wait()
        own_k = kv_ref[layer, group, :, 0].reshape(256, HEAD)
        own_v = widen(kv_ref[layer, group, :, 1].reshape(256, HEAD))
        for x in range(NX):
            rows = pl.ds(x * ROW_TILE, ROW_TILE)
            q = qx_ref[layer, x]
            if layer == 1:
                q = (q.astype(jnp.float32)
                     + gain_ref[...] * o_ref[0, x].astype(jnp.float32)).astype(jnp.bfloat16)
            q = jnp.concatenate([q[:, h * HEAD:(h + 1) * HEAD] for h in range(4)], axis=0)
            for half in range(2):
                qa[half, rows, :HEAD] = q
                qa[half, rows, HEAD:] = bias_ref[x, half]
            s = product(q, own_k)
            r = lax.broadcasted_iota(jnp.int32, s.shape, 0)
            t = lax.broadcasted_iota(jnp.int32, s.shape, 1)
            seen = (t // 32 == x * 2 + (r % 64) // 32) & (t % 32 <= r % 32)
            s = jnp.where(seen, s, MASKED)
            m = jnp.max(s, axis=1, keepdims=True)
            p = jnp.exp2((s - m) * LOG2_SCALE).astype(jnp.bfloat16)
            acc_s[rows, :] = jnp.dot(p, own_v, preferred_element_type=jnp.float32)
            m_s[rows, :] = jnp.broadcast_to(m, (ROW_TILE, HEAD))

        def step(j, _):
            per = KEY_TILE // 256
            k = kv_ref[layer, pl.ds(j * per, per), :, 0].reshape(KEY_TILE, HEAD)
            v = widen(kv_ref[layer, pl.ds(j * per, per), :, 1].reshape(KEY_TILE, HEAD))
            tiles = 4096 // KEY_TILE
            hot = hot_ref[pl.ds(pl.multiple_of(lax.rem(j, tiles) * KEY_TILE, KEY_TILE), KEY_TILE), :]
            k = jnp.concatenate([k, hot], axis=1)
            for x in range(1024 // ROW_TILE):
                rows = pl.ds(x * ROW_TILE, ROW_TILE)
                s = product(qa[j // tiles, rows, :], k)
                m_old = m_s[rows, :]
                m_new = jnp.maximum(m_old, jnp.max(s, axis=1, keepdims=True))
                a = jnp.exp2((m_old - m_new) * LOG2_SCALE)
                wide = jnp.concatenate([m_new] * (KEY_TILE // HEAD), axis=1)
                p = jnp.exp2((s - wide) * LOG2_SCALE).astype(jnp.bfloat16)
                acc_s[rows, :] = (acc_s[rows, :] * jnp.concatenate([a, a], axis=1)
                                  + jnp.dot(p, v, preferred_element_type=jnp.float32))
                m_s[rows, :] = m_new
            return 0

        lax.fori_loop(0, 8192 // KEY_TILE, step, 0)
        for x in range(NX):
            rows = pl.ds(x * ROW_TILE, ROW_TILE)
            out = (acc_s[rows, :HEAD] / acc_s[rows, HEAD:]).astype(jnp.bfloat16)
            o_ref[layer, x] = jnp.concatenate([out[h * 64:(h + 1) * 64] for h in range(4)], axis=1)


def attend(qx, kv, bias, hot, gain):
    vmem = pl.BlockSpec(memory_space=pltpu.VMEM)
    return pl.pallas_call(
        attend_kernel,
        out_shape=jax.ShapeDtypeStruct(qx.shape, jnp.bfloat16),
        in_specs=[vmem, pl.BlockSpec(memory_space=pl.ANY), vmem, vmem, vmem],
        out_specs=vmem,
        scratch_shapes=[
            pltpu.VMEM(kv.shape, jnp.bfloat16),
            pltpu.VMEM((2, 1024, 2 * HEAD), jnp.bfloat16),
            pltpu.VMEM((1024, HEAD), jnp.float32),
            pltpu.VMEM((1024, 2 * HEAD), jnp.float32),
            pltpu.SemaphoreType.DMA((2,)),
        ],
        compiler_params=pltpu.CompilerParams(vmem_limit_bytes=60 * 2**20),
    )(qx, kv, bias, hot, gain)


def return_kernel(o_ref, out_ref, send, recv, own_sem):
    section, ctx, group, x = here()
    greet([group_partner(section, group, x, step)[2] for step in range(1, 2 * NX)])
    columns = pl.ds(pl.multiple_of(x * 1024 + section * 512, 512), 512)
    copies = []
    for step in range(1, 2 * NX):
        layer, x_to, device = group_partner(section, group, x, step)
        copies.append(remote(o_ref.at[layer, x_to], out_ref.at[0, :, columns],
                             send.at[step - 1], recv.at[step - 1], device))
    for copy in copies:
        copy.start()
    own = pltpu.make_async_copy(o_ref.at[section, x], out_ref.at[0, :, columns], own_sem)
    own.start()
    own.wait()
    for copy in copies:
        copy.wait()


def give_back(o, rows):
    dma = pltpu.SemaphoreType.DMA
    any_spec = pl.BlockSpec(memory_space=pl.ANY)
    return pl.pallas_call(
        return_kernel,
        out_shape=jax.ShapeDtypeStruct((1, rows, 4096), jnp.bfloat16),
        in_specs=[any_spec],
        out_specs=any_spec,
        scratch_shapes=[dma((7,)), dma((7,)), dma],
        compiler_params=pltpu.CompilerParams(collective_id=1, has_side_effects=True),
    )(o)


def body(queries, key_rows, rows_of_value, query_gain, block_order):
    section, ctx, group, x = here()
    qx, kv = gather(queries, key_rows, rows_of_value)
    own = lax.dynamic_slice_in_dim(block_order, group * 8, 8, 0)
    hidden = block_order[None, :] >= own[:, None]
    bias = jnp.where(hidden, MASKED, 0.0).astype(jnp.bfloat16).reshape(4, 2, 2, 128)
    bias = jnp.transpose(bias, (0, 2, 1, 3))
    bias = jnp.broadcast_to(bias[:, :, None, :, None, :], (4, 2, 4, 2, 32, 128)).reshape(4, 2, 256, 128)
    key_block = lax.broadcasted_iota(jnp.int32, (4096, 128), 0) // 32
    hot = (key_block == lax.broadcasted_iota(jnp.int32, (4096, 128), 1)).astype(jnp.bfloat16)
    gain = lax.dynamic_slice_in_dim(query_gain, x * 1024 + section * 512, 512, 0)[None, :]
    o = attend(qx, kv, bias, hot, gain)
    return give_back(o, queries.shape[1])


def solution(mesh):
    placed = (
        P("section", "ctx", None),
        P("section", "ctx", None),
        P("section", "ctx", None),
        P(),
        P(),
    )
    return jax.shard_map(
        body, mesh=mesh, in_specs=placed, out_specs=P("section", "ctx", None), check_vma=False
    )
```

```python
import math

import jax
import jax.numpy as jnp
from jax import lax
from jax.experimental import pallas as pl
from jax.experimental.pallas import tpu as pltpu
from jax.sharding import PartitionSpec as P

MESH = pl.DeviceIdType.MESH
HEAD = 128
NX, NY, NZ = 4, 4, 8
GROUPS = NY * NZ
LOG2_SCALE = math.log2(math.e) / math.sqrt(HEAD)
MASKED = -1e30
CHUNK = 256
ROW_TILE = 256


def ring_events(na, nb):
    def offsets(n):
        return [0] + [s * d for d in range(1, n // 2) for s in (1, -1)] + [n // 2]

    events = [(a, b) for a in offsets(na) for b in offsets(nb)]
    return sorted(events, key=lambda e: (abs(e[0]) + abs(e[1]), abs(e[1])))


def here():
    section = lax.axis_index("section")
    ctx = lax.axis_index("ctx")
    return section, ctx, ctx // NX, ctx % NX


def greet(partners):
    barrier = pltpu.get_barrier_semaphore()
    for device in partners:
        pl.semaphore_signal(barrier, inc=1, device_id=device, device_id_type=MESH)
    pl.semaphore_wait(barrier, len(partners))


def remote(src, dst, send_sem, recv_sem, device):
    return pltpu.make_async_remote_copy(
        src_ref=src, dst_ref=dst, send_sem=send_sem, recv_sem=recv_sem,
        device_id=device, device_id_type=MESH,
    )


def group_partner(section, group, x, step):
    other = lax.rem(section * NX + x + step, 2 * NX)
    return other // NX, other % NX, (other // NX, group * NX + other % NX)


def layer_kernel(q_ref, k_ref, v_ref, gain_ref, order_ref, order_smem, out_ref,
                 kv, qx, hot, qa, m_s, acc_s, o_s, q_send, q_recv, x_send, x_recv,
                 ring_send, ring_recv, sib_send, sib_recv, own_sem, out_send, out_recv, out_own):
    section, ctx, group, x = here()
    y, z = group // NZ, group % NZ

    def at(y_at, z_at):
        return (section, (lax.rem(y_at + NY, NY) * NZ + lax.rem(z_at + NZ, NZ)) * NX + x)

    partners = [group_partner(section, group, x, step)[2] for step in range(1, 2 * NX)]
    greet(partners + [at(y + 1, z), at(y - 1, z), at(y, z + 1), at(y, z - 1)])

    exchanged = []
    for step in range(1, NX):
        x_to = lax.rem(x + step, NX)
        columns = pl.ds(pl.multiple_of(x_to * HEAD, HEAD), HEAD)
        for which, ref in ((0, k_ref), (1, v_ref)):
            copy = remote(
                ref.at[0, :, columns], kv.at[section, group, x, which],
                x_send.at[step - 1, which], x_recv.at[step - 1, which],
                (section, group * NX + x_to),
            )
            copy.start()
            exchanged.append(copy)
    own = []
    columns = pl.ds(pl.multiple_of(x * HEAD, HEAD), HEAD)
    for which, ref in ((0, k_ref), (1, v_ref)):
        own.append(pltpu.make_async_copy(
            ref.at[0, :, columns], kv.at[section, group, x, which], own_sem.at[which]))
    own.append(pltpu.make_async_copy(
        q_ref.at[0, :, pl.ds(pl.multiple_of(x * 1024 + section * 512, 512), 512)],
        qx.at[section, x], own_sem.at[2]))
    for copy in own:
        copy.start()
    moved = []
    for step in range(1, 2 * NX):
        core_to, x_to, device = group_partner(section, group, x, step)
        copy = remote(
            q_ref.at[0, :, pl.ds(pl.multiple_of(x_to * 1024 + core_to * 512, 512), 512)],
            qx.at[section, x], q_send.at[step - 1], q_recv.at[step - 1], device,
        )
        copy.start()
        moved.append(copy)
    for copy in own[:2]:
        copy.wait()
    for copy in exchanged:
        copy.wait_recv()

    def sibling_copy(layer, g, i):
        return remote(kv.at[layer, g], kv.at[layer, g], sib_send.at[i], sib_recv.at[i],
                      (1 - section, ctx))

    class Rings:
        def __init__(self, na, nb, z_first):
            self.na, self.nb, self.z_first = na, nb, z_first
            self.events = ring_events(na, nb)
            self.index = {e: i for i, e in enumerate(self.events)}

        def chunk(self, a, b):
            y_from, z_from = (y - b, z - a) if self.z_first else (y - a, z - b)
            return lax.rem(y_from + NY, NY) * NZ + lax.rem(z_from + NZ, NZ)

        def copy(self, g, event, half, da=0, db=1):
            slot = (self.index[event], 1 if half == 1 else 0)
            piece = kv.at[section, g] if half is None else kv.at[section, g, pl.ds(2 * half, 2)]
            device = at(y + db, z + da) if self.z_first else at(y + da, z + db)
            return remote(piece, piece, ring_send.at[slot], ring_recv.at[slot], device)

        def onward(self, event):
            a, b = event
            far_a, far_b = self.na // 2, self.nb // 2
            passed = []
            for sign in (1, -1):
                if b == 0 and a != far_a and a * sign >= 0:
                    to = a + sign
                    if abs(to) == far_a:
                        passed.append(((far_a, 0), 0 if sign > 0 else 1, sign, 0))
                    else:
                        passed.append(((to, 0), None, sign, 0))
            for sign in (1, -1):
                if b != far_b and b * sign >= 0:
                    to = b + sign
                    if abs(to) == far_b:
                        passed.append(((a, far_b), 0 if sign > 0 else 1, 0, sign))
                    else:
                        passed.append(((a, to), None, 0, sign))
            return passed

        def handle(self, i):
            a, b = event = self.events[i]
            g = self.chunk(a, b)
            if i:
                split = b == self.nb // 2 or (b == 0 and a == self.na // 2)
                for half in (0, 1) if split else (None,):
                    self.copy(g, event, half).wait_recv()
            for to, half, da, db in self.onward(event):
                self.copy(g, to, half, da, db).start()
            sibling_copy(section, g, i).start()

        def finish(self):
            for i, event in enumerate(self.events):
                g = self.chunk(*event)
                for to, half, da, db in self.onward(event):
                    self.copy(g, to, half, da, db).wait_send()
                sibling_copy(section, g, i).wait_send()

    first, second = Rings(NZ, NY, True), Rings(NY, NZ, False)

    def advance(indices):
        @pl.when(section == 0)
        def _():
            for i in indices:
                first.handle(i)

        @pl.when(section == 1)
        def _():
            for i in indices:
                second.handle(i)
            for i in indices:
                sibling_copy(0, first.chunk(*first.events[i]), i).wait_recv()

    def arrived(i):
        a, b = first.events[0]
        for n, event in enumerate(first.events[1:], 1):
            a, b = jnp.where(i == n, event[0], a), jnp.where(i == n, event[1], b)
        return first.chunk(a, b)

    advance([0])

    def fill_hot(i, _):
        block = lax.shift_right_logical(lax.broadcasted_iota(jnp.int32, (CHUNK, HEAD), 0), 5)
        lane = lax.broadcasted_iota(jnp.int32, (CHUNK, HEAD), 1)
        rows = pl.ds(pl.multiple_of(i * CHUNK, CHUNK), CHUNK)
        hot[rows, :] = jnp.where(block + i * 8 == lane, 1.0, 0.0).astype(jnp.bfloat16)
        return 0

    lax.fori_loop(0, 16, fill_hot, 0)
    for block in range(8):
        mine = order_smem[group * 8 + block]
        for half in range(2):
            order = jnp.broadcast_to(order_ref[:, half * HEAD:(half + 1) * HEAD], (32, HEAD))
            bias = jnp.where(order >= mine, MASKED, 0.0).astype(jnp.bfloat16)
            for h in range(4):
                qa[half, pl.ds(block // 2 * 256 + h * 64 + block % 2 * 32, 32), HEAD:] = bias
    own[2].wait()
    for copy in moved:
        copy.wait()
    for copy in exchanged:
        copy.wait_send()

    def widen(v):
        return jnp.concatenate([v, jnp.ones(v.shape, jnp.bfloat16)], axis=1)

    def product(q, k):
        return lax.dot_general(q, k, (((1,), (1,)), ((), ())), preferred_element_type=jnp.float32)

    def begin(layer):
        own_k = kv[layer, group, :, 0].reshape(CHUNK, HEAD)
        own_v = widen(kv[layer, group, :, 1].reshape(CHUNK, HEAD))
        for xs in range(NX):
            rows = pl.ds(xs * ROW_TILE, ROW_TILE)
            q = qx[layer, xs]
            if layer == 1:
                gain = gain_ref[:, pl.ds(pl.multiple_of(x * 1024 + section * 512, 512), 512)]
                q = (q.astype(jnp.float32)
                     + gain * o_s[0, xs].astype(jnp.float32)).astype(jnp.bfloat16)
            q = jnp.concatenate([q[:, h * HEAD:(h + 1) * HEAD] for h in range(4)], axis=0)
            for half in range(2):
                qa[half, rows, :HEAD] = q
            s = product(q, own_k)
            r = lax.broadcasted_iota(jnp.int32, s.shape, 0)
            t = lax.broadcasted_iota(jnp.int32, s.shape, 1)
            seen = (t // 32 == xs * 2 + (r % 64) // 32) & (t % 32 <= r % 32)
            s = jnp.where(seen, s, MASKED)
            m = jnp.max(s, axis=1, keepdims=True)
            p = jnp.exp2((s - m) * LOG2_SCALE).astype(jnp.bfloat16)
            acc_s[rows, :] = jnp.dot(p, own_v, preferred_element_type=jnp.float32)
            m_s[rows, :] = jnp.broadcast_to(m, (ROW_TILE, HEAD))

    def fold(layer, chunks):
        keys, values = [], []
        for g in chunks:
            k = kv[layer, g, :, 0].reshape(CHUNK, HEAD)
            rows = pl.ds(pl.multiple_of(lax.rem(g, 16) * CHUNK, CHUNK), CHUNK)
            keys.append(jnp.concatenate([k, hot[rows, :]], axis=1))
            values.append(kv[layer, g, :, 1].reshape(CHUNK, HEAD))
        v = widen(jnp.concatenate(values, axis=0))
        for xs in range(NX):
            rows = pl.ds(xs * ROW_TILE, ROW_TILE)
            s = jnp.concatenate(
                [product(qa[g // 16, rows, :], k) for g, k in zip(chunks, keys)], axis=1)
            m_old = m_s[rows, :]
            m_new = jnp.maximum(m_old, jnp.max(s, axis=1, keepdims=True))
            a = jnp.exp2((m_old - m_new) * LOG2_SCALE)
            wide = jnp.concatenate([m_new] * (s.shape[1] // HEAD), axis=1)
            p = jnp.exp2((s - wide) * LOG2_SCALE).astype(jnp.bfloat16)
            acc_s[rows, :] = (acc_s[rows, :] * jnp.concatenate([a, a], axis=1)
                              + jnp.dot(p, v, preferred_element_type=jnp.float32))
            m_s[rows, :] = m_new

    back = pl.ds(pl.multiple_of(x * 1024 + section * 512, 512), 512)

    def return_copy(layer, k):
        x_to = lax.rem(x + k, NX)
        return remote(o_s.at[layer, x_to], out_ref.at[0, :, back], out_send.at[layer, k],
                      out_recv.at[section, k], (layer, group * NX + x_to))

    def own_return():
        return pltpu.make_async_copy(o_s.at[section, x], out_ref.at[0, :, back], out_own)

    def end(layer):
        for xs in range(NX):
            rows = pl.ds(xs * ROW_TILE, ROW_TILE)
            out = (acc_s[rows, :HEAD] / acc_s[rows, HEAD:]).astype(jnp.bfloat16)
            o_s[layer, xs] = jnp.concatenate([out[h * 64:(h + 1) * 64] for h in range(4)], axis=1)

    def send_back(layer):
        for k in range(1, NX):
            return_copy(layer, k).start()

        @pl.when(section != layer)
        def _():
            return_copy(layer, 0).start()

        @pl.when(section == layer)
        def _():
            own_return().start()

    begin(0)

    def step0(j, _):
        for i in range(16):
            @pl.when(j == i)
            def _():
                advance([2 * i, 2 * i + 1] if i else [1])
        fold(0, [arrived(2 * j), arrived(2 * j + 1)])
        return 0

    lax.fori_loop(0, 16, step0, 0)
    end(0)

    @pl.when(section == 0)
    def _():
        for i, event in enumerate(second.events):
            sibling_copy(1, second.chunk(*event), i).wait_recv()

    begin(1)
    send_back(0)

    def step1(j, _):
        fold(1, [2 * j, 2 * j + 1])
        return 0

    lax.fori_loop(0, 16, step1, 0)
    end(1)
    send_back(1)

    @pl.when(section == 0)
    def _():
        first.finish()

    @pl.when(section == 1)
    def _():
        second.finish()

    own_return().wait()
    for core in range(2):
        for k in range(1, NX):
            return_copy(core, k).wait_send()
            remote(o_s.at[0, 0], out_ref.at[0, :, back], out_send.at[core, k],
                   out_recv.at[core, k], (1 - section, ctx)).wait_recv()

        @pl.when(section != core)
        def _():
            return_copy(core, 0).wait_send()
            remote(o_s.at[0, 0], out_ref.at[0, :, back], out_send.at[core, 0],
                   out_recv.at[core, 0], (1 - section, ctx)).wait_recv()


def body(queries, key_rows, rows_of_value, query_gain, block_order):
    rows = queries.shape[1]
    dma = pltpu.SemaphoreType.DMA
    hbm = pl.BlockSpec(memory_space=pl.ANY)
    vmem = pl.BlockSpec(memory_space=pltpu.VMEM)
    return pl.pallas_call(
        layer_kernel,
        out_shape=jax.ShapeDtypeStruct(queries.shape, jnp.bfloat16),
        in_specs=[hbm, hbm, hbm, vmem, vmem, pl.BlockSpec(memory_space=pltpu.SMEM)],
        out_specs=hbm,
        scratch_shapes=[
            pltpu.VMEM((2, GROUPS, NX, 2, rows, HEAD), jnp.bfloat16),
            pltpu.VMEM((2, NX, rows, 4 * HEAD), jnp.bfloat16),
            pltpu.VMEM((4096, HEAD), jnp.bfloat16),
            pltpu.VMEM((2, 1024, 2 * HEAD), jnp.bfloat16),
            pltpu.VMEM((1024, HEAD), jnp.float32),
            pltpu.VMEM((1024, 2 * HEAD), jnp.float32),
            pltpu.VMEM((2, NX, rows, 4 * HEAD), jnp.bfloat16),
            dma((7,)), dma((7,)), dma((3, 2)), dma((3, 2)), dma((32, 2)), dma((32, 2)),
            dma((32,)), dma((32,)), dma((3,)), dma((2, 4)), dma((2, 4)), dma,
        ],
        compiler_params=pltpu.CompilerParams(
            collective_id=0, has_side_effects=True, vmem_limit_bytes=60 * 2**20),
    )(queries, key_rows, rows_of_value, query_gain[None, :], block_order[None, :], block_order)


def solution(mesh):
    placed = (
        P("section", "ctx", None),
        P("section", "ctx", None),
        P("section", "ctx", None),
        P(),
        P(),
    )
    return jax.shard_map(
        body, mesh=mesh, in_specs=placed, out_specs=P("section", "ctx", None), check_vma=False
    )
```

```python
import math

import jax
import jax.numpy as jnp
from jax import lax
from jax.experimental import pallas as pl
from jax.experimental.pallas import tpu as pltpu
from jax.sharding import PartitionSpec as P

MESH = pl.DeviceIdType.MESH
HEAD = 128
NX, NY, NZ = 4, 4, 8
GROUPS = NY * NZ
LOG2_SCALE = math.log2(math.e) / math.sqrt(HEAD)
MASKED = -1e30
CHUNK = 256
ROW_TILE = 256


def ring_events(na, nb):
    def offsets(n):
        return [0] + [s * d for d in range(1, n // 2) for s in (1, -1)] + [n // 2]

    events = [(a, b) for a in offsets(na) for b in offsets(nb)]
    return sorted(events, key=lambda e: (abs(e[0]) + abs(e[1]), abs(e[1])))


def here():
    section = lax.axis_index("section")
    ctx = lax.axis_index("ctx")
    return section, ctx, ctx // NX, ctx % NX


def greet(partners):
    barrier = pltpu.get_barrier_semaphore()
    for device in partners:
        pl.semaphore_signal(barrier, inc=1, device_id=device, device_id_type=MESH)
    pl.semaphore_wait(barrier, len(partners))


def remote(src, dst, send_sem, recv_sem, device):
    return pltpu.make_async_remote_copy(
        src_ref=src, dst_ref=dst, send_sem=send_sem, recv_sem=recv_sem,
        device_id=device, device_id_type=MESH,
    )


def group_partner(section, group, x, step):
    other = lax.rem(section * NX + x + step, 2 * NX)
    return other // NX, other % NX, (other // NX, group * NX + other % NX)


def layer_kernel(q_ref, k_ref, v_ref, gain_ref, order_ref, order_smem, out_ref,
                 kv, qx, hot, qa, m_s, acc_s, o_s, q_send, q_recv, x_send, x_recv,
                 ring_send, ring_recv, sib_send, sib_recv, own_sem, out_send, out_recv, out_own):
    section, ctx, group, x = here()
    y, z = group // NZ, group % NZ

    def at(y_at, z_at):
        return (section, (lax.rem(y_at + NY, NY) * NZ + lax.rem(z_at + NZ, NZ)) * NX + x)

    partners = [group_partner(section, group, x, step)[2] for step in range(1, 2 * NX)]
    greet(partners + [at(y + 1, z), at(y - 1, z), at(y, z + 1), at(y, z - 1)])

    exchanged = []
    for step in range(1, NX):
        x_to = lax.rem(x + step, NX)
        columns = pl.ds(pl.multiple_of(x_to * HEAD, HEAD), HEAD)
        for which, ref in ((0, k_ref), (1, v_ref)):
            copy = remote(
                ref.at[0, :, columns], kv.at[section, group, x, which],
                x_send.at[step - 1, which], x_recv.at[step - 1, which],
                (section, group * NX + x_to),
            )
            copy.start()
            exchanged.append(copy)
    own = []
    columns = pl.ds(pl.multiple_of(x * HEAD, HEAD), HEAD)
    for which, ref in ((0, k_ref), (1, v_ref)):
        own.append(pltpu.make_async_copy(
            ref.at[0, :, columns], kv.at[section, group, x, which], own_sem.at[which]))
    own.append(pltpu.make_async_copy(
        q_ref.at[0, :, pl.ds(pl.multiple_of(x * 1024 + section * 512, 512), 512)],
        qx.at[section, x], own_sem.at[2]))
    for copy in own:
        copy.start()
    def query_copy(core_to, k):
        x_to = lax.rem(x + k, NX)
        return remote(
            q_ref.at[0, :, pl.ds(pl.multiple_of(x_to * 1024 + core_to * 512, 512), 512)],
            qx.at[section, x], q_send.at[core_to, k], q_recv.at[section, k],
            (core_to, group * NX + x_to),
        )

    def send_queries(layer):
        for core in range(2):
            for k in range(1, NX):
                query_copy(core, k).start()
        query_copy(1 - layer, 0).start()

    def wait_queries(layer):
        for k in range(1, NX):
            remote(qx.at[layer, x], qx.at[layer, x], q_send.at[0, k], q_recv.at[layer, k],
                   (1 - section, ctx)).wait_recv()

        @pl.when(section != layer)
        def _():
            remote(qx.at[layer, x], qx.at[layer, x], q_send.at[0, 0], q_recv.at[layer, 0],
                   (1 - section, ctx)).wait_recv()

    @pl.when(section == 0)
    def _():
        send_queries(0)

    for copy in own[:2]:
        copy.wait()
    for copy in exchanged:
        copy.wait_recv()

    def sibling_copy(layer, g, i):
        return remote(kv.at[layer, g], kv.at[layer, g], sib_send.at[i], sib_recv.at[i],
                      (1 - section, ctx))

    class Rings:
        def __init__(self, na, nb, z_first):
            self.na, self.nb, self.z_first = na, nb, z_first
            self.events = ring_events(na, nb)
            self.index = {e: i for i, e in enumerate(self.events)}

        def chunk(self, a, b):
            y_from, z_from = (y - b, z - a) if self.z_first else (y - a, z - b)
            return lax.rem(y_from + NY, NY) * NZ + lax.rem(z_from + NZ, NZ)

        def copy(self, g, event, half, da=0, db=1):
            slot = (self.index[event], 1 if half == 1 else 0)
            piece = kv.at[section, g] if half is None else kv.at[section, g, pl.ds(2 * half, 2)]
            device = at(y + db, z + da) if self.z_first else at(y + da, z + db)
            return remote(piece, piece, ring_send.at[slot], ring_recv.at[slot], device)

        def onward(self, event):
            a, b = event
            far_a, far_b = self.na // 2, self.nb // 2
            passed = []
            for sign in (1, -1):
                if b == 0 and a != far_a and a * sign >= 0:
                    to = a + sign
                    if abs(to) == far_a:
                        passed.append(((far_a, 0), 0 if sign > 0 else 1, sign, 0))
                    else:
                        passed.append(((to, 0), None, sign, 0))
            for sign in (1, -1):
                if b != far_b and b * sign >= 0:
                    to = b + sign
                    if abs(to) == far_b:
                        passed.append(((a, far_b), 0 if sign > 0 else 1, 0, sign))
                    else:
                        passed.append(((a, to), None, 0, sign))
            return passed

        def handle(self, i):
            a, b = event = self.events[i]
            g = self.chunk(a, b)
            if i:
                split = b == self.nb // 2 or (b == 0 and a == self.na // 2)
                for half in (0, 1) if split else (None,):
                    self.copy(g, event, half).wait_recv()
            for to, half, da, db in self.onward(event):
                self.copy(g, to, half, da, db).start()
            sibling_copy(section, g, i).start()

        def finish(self):
            for i, event in enumerate(self.events):
                g = self.chunk(*event)
                for to, half, da, db in self.onward(event):
                    self.copy(g, to, half, da, db).wait_send()
                sibling_copy(section, g, i).wait_send()

    first, second = Rings(NZ, NY, True), Rings(NY, NZ, False)

    def advance(indices):
        @pl.when(section == 0)
        def _():
            for i in indices:
                first.handle(i)

        @pl.when(section == 1)
        def _():
            for i in indices:
                second.handle(i)
            for i in indices:
                sibling_copy(0, first.chunk(*first.events[i]), i).wait_recv()

    def arrived(i):
        a, b = first.events[0]
        for n, event in enumerate(first.events[1:], 1):
            a, b = jnp.where(i == n, event[0], a), jnp.where(i == n, event[1], b)
        return first.chunk(a, b)

    advance([0])

    def fill_hot(i, _):
        block = lax.shift_right_logical(lax.broadcasted_iota(jnp.int32, (CHUNK, HEAD), 0), 5)
        lane = lax.broadcasted_iota(jnp.int32, (CHUNK, HEAD), 1)
        rows = pl.ds(pl.multiple_of(i * CHUNK, CHUNK), CHUNK)
        hot[rows, :] = jnp.where(block + i * 8 == lane, 1.0, 0.0).astype(jnp.bfloat16)
        return 0

    lax.fori_loop(0, 16, fill_hot, 0)
    for block in range(8):
        mine = order_smem[group * 8 + block]
        for half in range(2):
            order = jnp.broadcast_to(order_ref[:, half * HEAD:(half + 1) * HEAD], (32, HEAD))
            bias = jnp.where(order >= mine, MASKED, 0.0).astype(jnp.bfloat16)
            for h in range(4):
                qa[half, pl.ds(block // 2 * 256 + h * 64 + block % 2 * 32, 32), HEAD:] = bias
    own[2].wait()
    wait_queries(0)
    for copy in exchanged:
        copy.wait_send()

    def widen(v):
        return jnp.concatenate([v, jnp.ones(v.shape, jnp.bfloat16)], axis=1)

    def product(q, k):
        return lax.dot_general(q, k, (((1,), (1,)), ((), ())), preferred_element_type=jnp.float32)

    def begin(layer):
        own_k = kv[layer, group, :, 0].reshape(CHUNK, HEAD)
        own_v = widen(kv[layer, group, :, 1].reshape(CHUNK, HEAD))
        for xs in range(NX):
            rows = pl.ds(xs * ROW_TILE, ROW_TILE)
            q = qx[layer, xs]
            if layer == 1:
                gain = gain_ref[:, pl.ds(pl.multiple_of(x * 1024 + section * 512, 512), 512)]
                q = (q.astype(jnp.float32)
                     + gain * o_s[0, xs].astype(jnp.float32)).astype(jnp.bfloat16)
            q = jnp.concatenate([q[:, h * HEAD:(h + 1) * HEAD] for h in range(4)], axis=0)
            for half in range(2):
                qa[half, rows, :HEAD] = q
            s = product(q, own_k)
            r = lax.broadcasted_iota(jnp.int32, s.shape, 0)
            t = lax.broadcasted_iota(jnp.int32, s.shape, 1)
            seen = (t // 32 == xs * 2 + (r % 64) // 32) & (t % 32 <= r % 32)
            s = jnp.where(seen, s, MASKED)
            m = jnp.max(s, axis=1, keepdims=True)
            p = jnp.exp2((s - m) * LOG2_SCALE).astype(jnp.bfloat16)
            acc_s[rows, :] = jnp.dot(p, own_v, preferred_element_type=jnp.float32)
            m_s[rows, :] = jnp.broadcast_to(m, (ROW_TILE, HEAD))

    def fold(layer, chunk_groups, tiles):
        operands = []
        for chunks in chunk_groups:
            keys, values = [], []
            for g in chunks:
                k = kv[layer, g, :, 0].reshape(CHUNK, HEAD)
                rows = pl.ds(pl.multiple_of(lax.rem(g, 16) * CHUNK, CHUNK), CHUNK)
                keys.append(jnp.concatenate([k, hot[rows, :]], axis=1))
                values.append(kv[layer, g, :, 1].reshape(CHUNK, HEAD))
            operands.append((chunks, keys, widen(jnp.concatenate(values, axis=0))))
        items = [(operand, pl.ds(xs * ROW_TILE, ROW_TILE)) for operand in operands for xs in tiles]

        def scores(item):
            (chunks, keys, _), rows = item
            return jnp.concatenate(
                [product(qa[g // 16, rows, :], k) for g, k in zip(chunks, keys)], axis=1)

        def update(item, s):
            (_, _, v), rows = item
            m_old = m_s[rows, :]
            m_new = jnp.maximum(m_old, jnp.max(s, axis=1, keepdims=True))
            a = jnp.exp2((m_old - m_new) * LOG2_SCALE)
            wide = jnp.concatenate([m_new] * (s.shape[1] // HEAD), axis=1)
            p = jnp.exp2((s - wide) * LOG2_SCALE).astype(jnp.bfloat16)
            acc_s[rows, :] = (acc_s[rows, :] * jnp.concatenate([a, a], axis=1)
                              + jnp.dot(p, v, preferred_element_type=jnp.float32))
            m_s[rows, :] = m_new

        s = scores(items[0])
        for i, item in enumerate(items):
            later = scores(items[i + 1]) if i + 1 < len(items) else None
            update(item, s)
            s = later

    back = pl.ds(pl.multiple_of(x * 1024 + section * 512, 512), 512)

    def return_copy(layer, x_to):
        k = lax.rem(x_to + NX - x, NX)
        return remote(o_s.at[layer, x_to], out_ref.at[0, :, back], out_send.at[layer, x_to],
                      out_recv.at[section, k], (layer, group * NX + x_to))

    def own_return():
        return pltpu.make_async_copy(o_s.at[section, x], out_ref.at[0, :, back], out_own)

    def end(layer, tiles):
        for xs in tiles:
            rows = pl.ds(xs * ROW_TILE, ROW_TILE)
            out = (acc_s[rows, :HEAD] / acc_s[rows, HEAD:]).astype(jnp.bfloat16)
            o_s[layer, xs] = jnp.concatenate([out[h * 64:(h + 1) * 64] for h in range(4)], axis=1)

    def send_back(layer, tiles):
        for x_to in tiles:
            stays = (section == layer) & (x == x_to)

            @pl.when(jnp.logical_not(stays))
            def _():
                return_copy(layer, x_to).start()

            @pl.when(stays)
            def _():
                own_return().start()

    begin(0)
    advance([1, 2, 3])

    def step0(j, _):
        chunks = [arrived(4 * j + i) for i in range(4)]
        for half in range(2):
            fold(0, [chunks], (2 * half, 2 * half + 1))
            for i in range(7):
                @pl.when(j == i)
                def _():
                    advance([4 * i + 4 + 2 * half, 4 * i + 5 + 2 * half])

        @pl.when((j == 1) & (section == 1))
        def _():
            send_queries(1)

        return 0

    lax.fori_loop(0, 8, step0, 0)
    end(0, range(NX))

    @pl.when(section == 0)
    def _():
        for i, event in enumerate(second.events):
            sibling_copy(1, second.chunk(*event), i).wait_recv()

    wait_queries(1)
    begin(1)
    send_back(0, range(NX))

    for tiles in ((0, 1), (2, 3)):
        def step1(j, _):
            fold(1, [[8 * j + 4 * i + c for c in range(4)] for i in range(2)], tiles)
            return 0

        lax.fori_loop(0, 4, step1, 0)
        end(1, tiles)
        send_back(1, tiles)

    @pl.when(section == 0)
    def _():
        first.finish()

    @pl.when(section == 1)
    def _():
        second.finish()

    for core in range(2):
        for k in range(1, NX):
            query_copy(core, k).wait_send()
    query_copy(1 - section, 0).wait_send()
    own_return().wait()
    for layer in range(2):
        for x_to in range(NX):
            @pl.when(jnp.logical_not((section == layer) & (x == x_to)))
            def _():
                return_copy(layer, x_to).wait_send()
    for core in range(2):
        for k in range(1, NX):
            remote(o_s.at[0, 0], out_ref.at[0, :, back], out_send.at[core, k],
                   out_recv.at[core, k], (1 - section, ctx)).wait_recv()

        @pl.when(section != core)
        def _():
            remote(o_s.at[0, 0], out_ref.at[0, :, back], out_send.at[core, 0],
                   out_recv.at[core, 0], (1 - section, ctx)).wait_recv()


def body(queries, key_rows, rows_of_value, query_gain, block_order):
    rows = queries.shape[1]
    dma = pltpu.SemaphoreType.DMA
    hbm = pl.BlockSpec(memory_space=pl.ANY)
    vmem = pl.BlockSpec(memory_space=pltpu.VMEM)
    return pl.pallas_call(
        layer_kernel,
        out_shape=jax.ShapeDtypeStruct(queries.shape, jnp.bfloat16),
        in_specs=[hbm, hbm, hbm, vmem, vmem, pl.BlockSpec(memory_space=pltpu.SMEM)],
        out_specs=hbm,
        scratch_shapes=[
            pltpu.VMEM((2, GROUPS, NX, 2, rows, HEAD), jnp.bfloat16),
            pltpu.VMEM((2, NX, rows, 4 * HEAD), jnp.bfloat16),
            pltpu.VMEM((4096, HEAD), jnp.bfloat16),
            pltpu.VMEM((2, 1024, 2 * HEAD), jnp.bfloat16),
            pltpu.VMEM((1024, HEAD), jnp.float32),
            pltpu.VMEM((1024, 2 * HEAD), jnp.float32),
            pltpu.VMEM((2, NX, rows, 4 * HEAD), jnp.bfloat16),
            dma((2, 4)), dma((2, 4)), dma((3, 2)), dma((3, 2)), dma((32, 2)), dma((32, 2)),
            dma((32,)), dma((32,)), dma((3,)), dma((2, 4)), dma((2, 4)), dma,
        ],
        compiler_params=pltpu.CompilerParams(
            collective_id=0, has_side_effects=True, vmem_limit_bytes=60 * 2**20),
    )(queries, key_rows, rows_of_value, query_gain[None, :], block_order[None, :], block_order)


def solution(mesh):
    placed = (
        P("section", "ctx", None),
        P("section", "ctx", None),
        P("section", "ctx", None),
        P(),
        P(),
    )
    return jax.shard_map(
        body, mesh=mesh, in_specs=placed, out_specs=P("section", "ctx", None), check_vma=False
    )
```

```python
import math

import jax
import jax.numpy as jnp
from jax import lax
from jax.experimental import pallas as pl
from jax.experimental.pallas import tpu as pltpu
from jax.sharding import PartitionSpec as P

MESH = pl.DeviceIdType.MESH
HEAD = 128
NX, NY, NZ = 4, 4, 8
GROUPS = NY * NZ
LOG2_SCALE = math.log2(math.e) / math.sqrt(HEAD)
MASKED = -1e30
CHUNK = 256
ROW_TILE = 256


def ring_events(na, nb):
    def offsets(n):
        return [0] + [s * d for d in range(1, n // 2) for s in (1, -1)] + [n // 2]

    events = [(a, b) for a in offsets(na) for b in offsets(nb)]
    return sorted(events, key=lambda e: (abs(e[0]) + abs(e[1]), abs(e[1])))


def here():
    section = lax.axis_index("section")
    ctx = lax.axis_index("ctx")
    return section, ctx, ctx // NX, ctx % NX


def greet(partners):
    barrier = pltpu.get_barrier_semaphore()
    for device in partners:
        pl.semaphore_signal(barrier, inc=1, device_id=device, device_id_type=MESH)
    pl.semaphore_wait(barrier, len(partners))


def remote(src, dst, send_sem, recv_sem, device):
    return pltpu.make_async_remote_copy(
        src_ref=src, dst_ref=dst, send_sem=send_sem, recv_sem=recv_sem,
        device_id=device, device_id_type=MESH,
    )


def group_partner(section, group, x, step):
    other = lax.rem(section * NX + x + step, 2 * NX)
    return other // NX, other % NX, (other // NX, group * NX + other % NX)


def layer_kernel(q_ref, k_ref, v_ref, gain_ref, order_ref, order_smem, out_ref,
                 kv, qx, hot, qa, m_s, acc_s, o_s, q_send, q_recv, x_send, x_recv,
                 ring_send, ring_recv, sib_send, sib_recv, own_sem, out_send, out_recv, out_own):
    section, ctx, group, x = here()
    y, z = group // NZ, group % NZ

    def at(y_at, z_at):
        return (section, (lax.rem(y_at + NY, NY) * NZ + lax.rem(z_at + NZ, NZ)) * NX + x)

    partners = [group_partner(section, group, x, step)[2] for step in range(1, 2 * NX)]
    greet(partners + [at(y + 1, z), at(y - 1, z), at(y, z + 1), at(y, z - 1)])

    exchanged = []
    for step in range(1, NX):
        x_to = lax.rem(x + step, NX)
        columns = pl.ds(pl.multiple_of(x_to * HEAD, HEAD), HEAD)
        for which, ref in ((0, k_ref), (1, v_ref)):
            copy = remote(
                ref.at[0, :, columns], kv.at[section, group, x, which],
                x_send.at[step - 1, which], x_recv.at[step - 1, which],
                (section, group * NX + x_to),
            )
            copy.start()
            exchanged.append(copy)
    own = []
    columns = pl.ds(pl.multiple_of(x * HEAD, HEAD), HEAD)
    for which, ref in ((0, k_ref), (1, v_ref)):
        own.append(pltpu.make_async_copy(
            ref.at[0, :, columns], kv.at[section, group, x, which], own_sem.at[which]))
    own.append(pltpu.make_async_copy(
        q_ref.at[0, :, pl.ds(pl.multiple_of(x * 1024 + section * 512, 512), 512)],
        qx.at[section, x], own_sem.at[2]))
    for copy in own:
        copy.start()
    def query_copy(core_to, k):
        x_to = lax.rem(x + k, NX)
        return remote(
            q_ref.at[0, :, pl.ds(pl.multiple_of(x_to * 1024 + core_to * 512, 512), 512)],
            qx.at[section, x], q_send.at[core_to, k], q_recv.at[section, k],
            (core_to, group * NX + x_to),
        )

    def send_queries(layer):
        for core in range(2):
            for k in range(1, NX):
                query_copy(core, k).start()
        query_copy(1 - layer, 0).start()

    def wait_queries(layer):
        for k in range(1, NX):
            remote(qx.at[layer, x], qx.at[layer, x], q_send.at[0, k], q_recv.at[layer, k],
                   (1 - section, ctx)).wait_recv()

        @pl.when(section != layer)
        def _():
            remote(qx.at[layer, x], qx.at[layer, x], q_send.at[0, 0], q_recv.at[layer, 0],
                   (1 - section, ctx)).wait_recv()

    @pl.when(section == 0)
    def _():
        send_queries(0)

    def fill_hot(i, _):
        block = lax.shift_right_logical(lax.broadcasted_iota(jnp.int32, (CHUNK, HEAD), 0), 5)
        lane = lax.broadcasted_iota(jnp.int32, (CHUNK, HEAD), 1)
        rows = pl.ds(pl.multiple_of(i * CHUNK, CHUNK), CHUNK)
        hot[rows, :] = jnp.where(block + i * 8 == lane, 1.0, 0.0).astype(jnp.bfloat16)
        return 0

    lax.fori_loop(0, 16, fill_hot, 0)
    for block in range(8):
        mine = order_smem[group * 8 + block]
        for half in range(2):
            order = jnp.broadcast_to(order_ref[:, half * HEAD:(half + 1) * HEAD], (32, HEAD))
            bias = jnp.where(order >= mine, MASKED, 0.0).astype(jnp.bfloat16)
            for h in range(4):
                qa[half, pl.ds(block // 2 * 256 + h * 64 + block % 2 * 32, 32), HEAD:] = bias

    for copy in own[:2]:
        copy.wait()
    for copy in exchanged:
        copy.wait_recv()

    def sibling_copy(layer, g, i):
        return remote(kv.at[layer, g], kv.at[layer, g], sib_send.at[i], sib_recv.at[i],
                      (1 - section, ctx))

    class Rings:
        def __init__(self, na, nb, z_first):
            self.na, self.nb, self.z_first = na, nb, z_first
            self.events = ring_events(na, nb)
            self.index = {e: i for i, e in enumerate(self.events)}

        def chunk(self, a, b):
            y_from, z_from = (y - b, z - a) if self.z_first else (y - a, z - b)
            return lax.rem(y_from + NY, NY) * NZ + lax.rem(z_from + NZ, NZ)

        def copy(self, g, event, half, da=0, db=1):
            slot = (self.index[event], 1 if half == 1 else 0)
            piece = kv.at[section, g] if half is None else kv.at[section, g, pl.ds(2 * half, 2)]
            device = at(y + db, z + da) if self.z_first else at(y + da, z + db)
            return remote(piece, piece, ring_send.at[slot], ring_recv.at[slot], device)

        def onward(self, event):
            a, b = event
            far_a, far_b = self.na // 2, self.nb // 2
            passed = []
            for sign in (1, -1):
                if b == 0 and a != far_a and a * sign >= 0:
                    to = a + sign
                    if abs(to) == far_a:
                        passed.append(((far_a, 0), 0 if sign > 0 else 1, sign, 0))
                    else:
                        passed.append(((to, 0), None, sign, 0))
            for sign in (1, -1):
                if b != far_b and b * sign >= 0:
                    to = b + sign
                    if abs(to) == far_b:
                        passed.append(((a, far_b), 0 if sign > 0 else 1, 0, sign))
                    else:
                        passed.append(((a, to), None, 0, sign))
            return passed

        def handle(self, i):
            a, b = event = self.events[i]
            g = self.chunk(a, b)
            if i:
                split = b == self.nb // 2 or (b == 0 and a == self.na // 2)
                for half in (0, 1) if split else (None,):
                    self.copy(g, event, half).wait_recv()
            for to, half, da, db in self.onward(event):
                self.copy(g, to, half, da, db).start()
            sibling_copy(section, g, i).start()

        def finish(self):
            for i, event in enumerate(self.events):
                g = self.chunk(*event)
                for to, half, da, db in self.onward(event):
                    self.copy(g, to, half, da, db).wait_send()
                sibling_copy(section, g, i).wait_send()

    first, second = Rings(NZ, NY, True), Rings(NY, NZ, False)

    def advance(indices):
        @pl.when(section == 0)
        def _():
            for i in indices:
                first.handle(i)

        @pl.when(section == 1)
        def _():
            for i in indices:
                second.handle(i)
            for i in indices:
                sibling_copy(0, first.chunk(*first.events[i]), i).wait_recv()

    def arrived(j):
        packed = [[(e[0] + 8) * 16 + e[1] + 8 for e in first.events[c::4]] for c in range(4)]
        places = [jnp.int32(row[0]) for row in packed]
        for n in range(1, 8):
            now = j == n
            places = [jnp.where(now, row[n], place) for row, place in zip(packed, places)]
        return [first.chunk(place // 16 - 8, place % 16 - 8) for place in places]

    advance([0])
    advance([1, 2, 3, 4])
    own[2].wait()
    wait_queries(0)
    for copy in exchanged:
        copy.wait_send()

    def widen(v):
        return jnp.concatenate([v, jnp.ones(v.shape, jnp.bfloat16)], axis=1)

    def product(q, k):
        return lax.dot_general(q, k, (((1,), (1,)), ((), ())), preferred_element_type=jnp.float32)

    def begin(layer):
        for xs in range(NX):
            rows = pl.ds(xs * ROW_TILE, ROW_TILE)
            q = qx[layer, xs]
            if layer == 1:
                gain = gain_ref[:, pl.ds(pl.multiple_of(x * 1024 + section * 512, 512), 512)]
                q = (q.astype(jnp.float32)
                     + gain * o_s[0, xs].astype(jnp.float32)).astype(jnp.bfloat16)
            q = jnp.concatenate([q[:, h * HEAD:(h + 1) * HEAD] for h in range(4)], axis=0)
            for half in range(2):
                qa[half, rows, :HEAD] = q
            pair = pl.ds(xs // 2 * 2, 2)
            own_k = kv[layer, group, pair, 0].reshape(CHUNK // 2, HEAD)
            own_v = widen(kv[layer, group, pair, 1].reshape(CHUNK // 2, HEAD))
            s = product(q, own_k)
            r = lax.broadcasted_iota(jnp.int32, s.shape, 0)
            t = lax.broadcasted_iota(jnp.int32, s.shape, 1)
            seen = (t // 32 == xs % 2 * 2 + (r % 64) // 32) & (t % 32 <= r % 32)
            s = jnp.where(seen, s, MASKED)
            m = jnp.max(s, axis=1, keepdims=True)
            p = jnp.exp2((s - m) * LOG2_SCALE).astype(jnp.bfloat16)
            acc_s[rows, :] = jnp.dot(p, own_v, preferred_element_type=jnp.float32)
            m_s[rows, :] = jnp.broadcast_to(m, (ROW_TILE, HEAD))

    def fold(layer, chunk_groups, tiles):
        operands = []
        for chunks in chunk_groups:
            keys, values = [], []
            for g in chunks:
                k = kv[layer, g, :, 0].reshape(CHUNK, HEAD)
                rows = pl.ds(pl.multiple_of(lax.rem(g, 16) * CHUNK, CHUNK), CHUNK)
                keys.append(jnp.concatenate([k, hot[rows, :]], axis=1))
                values.append(kv[layer, g, :, 1].reshape(CHUNK, HEAD))
            operands.append((chunks, keys, widen(jnp.concatenate(values, axis=0))))
        items = [(operand, pl.ds(xs * ROW_TILE, ROW_TILE)) for operand in operands for xs in tiles]

        def scores(item):
            (chunks, keys, _), rows = item
            return jnp.concatenate(
                [product(qa[g // 16, rows, :], k) for g, k in zip(chunks, keys)], axis=1)

        def update(item, s):
            (_, _, v), rows = item
            m_old = m_s[rows, :]
            m_new = jnp.maximum(m_old, jnp.max(s, axis=1, keepdims=True))
            a = jnp.exp2((m_old - m_new) * LOG2_SCALE)
            wide = jnp.concatenate([m_new] * (s.shape[1] // HEAD), axis=1)
            p = jnp.exp2((s - wide) * LOG2_SCALE).astype(jnp.bfloat16)
            acc_s[rows, :] = (acc_s[rows, :] * jnp.concatenate([a, a], axis=1)
                              + jnp.dot(p, v, preferred_element_type=jnp.float32))
            m_s[rows, :] = m_new

        s = scores(items[0])
        for i, item in enumerate(items):
            later = scores(items[i + 1]) if i + 1 < len(items) else None
            update(item, s)
            s = later

    back = pl.ds(pl.multiple_of(x * 1024 + section * 512, 512), 512)

    def return_copy(layer, x_to):
        k = lax.rem(x_to + NX - x, NX)
        return remote(o_s.at[layer, x_to], out_ref.at[0, :, back], out_send.at[layer, x_to],
                      out_recv.at[section, k], (layer, group * NX + x_to))

    def own_return():
        return pltpu.make_async_copy(o_s.at[section, x], out_ref.at[0, :, back], out_own)

    def end(layer, tiles):
        for xs in tiles:
            rows = pl.ds(xs * ROW_TILE, ROW_TILE)
            out = (acc_s[rows, :HEAD] / acc_s[rows, HEAD:]).astype(jnp.bfloat16)
            o_s[layer, xs] = jnp.concatenate([out[h * 64:(h + 1) * 64] for h in range(4)], axis=1)

    def send_back(layer, tiles):
        for x_to in tiles:
            stays = (section == layer) & (x == x_to)

            @pl.when(jnp.logical_not(stays))
            def _():
                return_copy(layer, x_to).start()

            @pl.when(stays)
            def _():
                own_return().start()

    begin(0)

    def step0(j, _):
        chunks = arrived(j)
        for half in range(2):
            fold(0, [chunks], (2 * half, 2 * half + 1))
            for i in range(7):
                @pl.when(j == i)
                def _():
                    advance([e for e in (4 * i + 4 + 2 * half, 4 * i + 5 + 2 * half) if e > 4])

        @pl.when((j == 1) & (section == 1))
        def _():
            send_queries(1)

        return 0

    lax.fori_loop(0, 8, step0, 0)
    end(0, range(NX))

    @pl.when(section == 0)
    def _():
        for i, event in enumerate(second.events):
            sibling_copy(1, second.chunk(*event), i).wait_recv()

    wait_queries(1)
    begin(1)
    send_back(0, range(NX))

    for tiles in ((0, 1), (2, 3)):
        def step1(j, _):
            fold(1, [[8 * j + 4 * i + c for c in range(4)] for i in range(2)], tiles)
            return 0

        lax.fori_loop(0, 4, step1, 0)
        end(1, tiles)
        send_back(1, tiles)

    @pl.when(section == 0)
    def _():
        first.finish()

    @pl.when(section == 1)
    def _():
        second.finish()

    for core in range(2):
        for k in range(1, NX):
            query_copy(core, k).wait_send()
    query_copy(1 - section, 0).wait_send()
    own_return().wait()
    for layer in range(2):
        for x_to in range(NX):
            @pl.when(jnp.logical_not((section == layer) & (x == x_to)))
            def _():
                return_copy(layer, x_to).wait_send()
    for core in range(2):
        for k in range(1, NX):
            remote(o_s.at[0, 0], out_ref.at[0, :, back], out_send.at[core, k],
                   out_recv.at[core, k], (1 - section, ctx)).wait_recv()

        @pl.when(section != core)
        def _():
            remote(o_s.at[0, 0], out_ref.at[0, :, back], out_send.at[core, 0],
                   out_recv.at[core, 0], (1 - section, ctx)).wait_recv()


def body(queries, key_rows, rows_of_value, query_gain, block_order):
    rows = queries.shape[1]
    dma = pltpu.SemaphoreType.DMA
    hbm = pl.BlockSpec(memory_space=pl.ANY)
    vmem = pl.BlockSpec(memory_space=pltpu.VMEM)
    return pl.pallas_call(
        layer_kernel,
        out_shape=jax.ShapeDtypeStruct(queries.shape, jnp.bfloat16),
        in_specs=[hbm, hbm, hbm, vmem, vmem, pl.BlockSpec(memory_space=pltpu.SMEM)],
        out_specs=hbm,
        scratch_shapes=[
            pltpu.VMEM((2, GROUPS, NX, 2, rows, HEAD), jnp.bfloat16),
            pltpu.VMEM((2, NX, rows, 4 * HEAD), jnp.bfloat16),
            pltpu.VMEM((4096, HEAD), jnp.bfloat16),
            pltpu.VMEM((2, 1024, 2 * HEAD), jnp.bfloat16),
            pltpu.VMEM((1024, HEAD), jnp.float32),
            pltpu.VMEM((1024, 2 * HEAD), jnp.float32),
            pltpu.VMEM((2, NX, rows, 4 * HEAD), jnp.bfloat16),
            dma((2, 4)), dma((2, 4)), dma((3, 2)), dma((3, 2)), dma((32, 2)), dma((32, 2)),
            dma((32,)), dma((32,)), dma((3,)), dma((2, 4)), dma((2, 4)), dma,
        ],
        compiler_params=pltpu.CompilerParams(
            collective_id=0, has_side_effects=True, vmem_limit_bytes=60 * 2**20),
    )(queries, key_rows, rows_of_value, query_gain[None, :], block_order[None, :], block_order)


def solution(mesh):
    placed = (
        P("section", "ctx", None),
        P("section", "ctx", None),
        P("section", "ctx", None),
        P(),
        P(),
    )
    return jax.shard_map(
        body, mesh=mesh, in_specs=placed, out_specs=P("section", "ctx", None), check_vma=False
    )
```

```python
import math

import jax
import jax.numpy as jnp
from jax import lax
from jax.experimental import pallas as pl
from jax.experimental.pallas import tpu as pltpu
from jax.sharding import PartitionSpec as P

MESH = pl.DeviceIdType.MESH
HEAD = 128
NX, NY, NZ = 4, 4, 8
GROUPS = NY * NZ
LOG2_SCALE = math.log2(math.e) / math.sqrt(HEAD)
MASKED = -1e30
CHUNK = 256
ROW_TILE = 256


def ring_events(na, nb):
    def offsets(n):
        return [0] + [s * d for d in range(1, n // 2) for s in (1, -1)] + [n // 2]

    events = [(a, b) for a in offsets(na) for b in offsets(nb)]
    return sorted(events, key=lambda e: (abs(e[0]) + abs(e[1]), abs(e[1])))


def here():
    section = lax.axis_index("section")
    ctx = lax.axis_index("ctx")
    return section, ctx, ctx // NX, ctx % NX


def greet(partners):
    barrier = pltpu.get_barrier_semaphore()
    for device in partners:
        pl.semaphore_signal(barrier, inc=1, device_id=device, device_id_type=MESH)
    pl.semaphore_wait(barrier, len(partners))


def remote(src, dst, send_sem, recv_sem, device):
    return pltpu.make_async_remote_copy(
        src_ref=src, dst_ref=dst, send_sem=send_sem, recv_sem=recv_sem,
        device_id=device, device_id_type=MESH,
    )


def group_partner(section, group, x, step):
    other = lax.rem(section * NX + x + step, 2 * NX)
    return other // NX, other % NX, (other // NX, group * NX + other % NX)


def layer_kernel(q_ref, k_ref, v_ref, gain_ref, order_ref, order_smem, out_ref,
                 kv, qx, hot, qa, m_s, acc_s, o_s, q_send, q_recv, x_send, x_recv,
                 ring_send, ring_recv, sib_send, sib_recv, own_sem, out_send, out_recv, out_own):
    section, ctx, group, x = here()
    y, z = group // NZ, group % NZ

    def at(y_at, z_at):
        return (section, (lax.rem(y_at + NY, NY) * NZ + lax.rem(z_at + NZ, NZ)) * NX + x)

    partners = [group_partner(section, group, x, step)[2] for step in range(1, 2 * NX)]
    greet(partners + [at(y + 1, z), at(y - 1, z), at(y, z + 1), at(y, z - 1)])

    exchanged = []
    for step in range(1, NX):
        x_to = lax.rem(x + step, NX)
        columns = pl.ds(pl.multiple_of(x_to * HEAD, HEAD), HEAD)
        for which, ref in ((0, k_ref), (1, v_ref)):
            copy = remote(
                ref.at[0, :, columns], kv.at[section, group, x, which],
                x_send.at[step - 1, which], x_recv.at[step - 1, which],
                (section, group * NX + x_to),
            )
            copy.start()
            exchanged.append(copy)
    own = []
    columns = pl.ds(pl.multiple_of(x * HEAD, HEAD), HEAD)
    for which, ref in ((0, k_ref), (1, v_ref)):
        own.append(pltpu.make_async_copy(
            ref.at[0, :, columns], kv.at[section, group, x, which], own_sem.at[which]))
    own.append(pltpu.make_async_copy(
        q_ref.at[0, :, pl.ds(pl.multiple_of(x * 1024 + section * 512, 512), 512)],
        qx.at[section, x], own_sem.at[2]))
    for copy in own:
        copy.start()
    def query_copy(core_to, k):
        x_to = lax.rem(x + k, NX)
        return remote(
            q_ref.at[0, :, pl.ds(pl.multiple_of(x_to * 1024 + core_to * 512, 512), 512)],
            qx.at[section, x], q_send.at[core_to, k], q_recv.at[section, k],
            (core_to, group * NX + x_to),
        )

    def send_queries(layer):
        for core in range(2):
            for k in range(1, NX):
                query_copy(core, k).start()
        query_copy(1 - layer, 0).start()

    def wait_queries(layer):
        for k in range(1, NX):
            remote(qx.at[layer, x], qx.at[layer, x], q_send.at[0, k], q_recv.at[layer, k],
                   (1 - section, ctx)).wait_recv()

        @pl.when(section != layer)
        def _():
            remote(qx.at[layer, x], qx.at[layer, x], q_send.at[0, 0], q_recv.at[layer, 0],
                   (1 - section, ctx)).wait_recv()

    @pl.when(section == 0)
    def _():
        send_queries(0)

    def fill_hot(i, _):
        block = lax.shift_right_logical(lax.broadcasted_iota(jnp.int32, (CHUNK, HEAD), 0), 5)
        lane = lax.broadcasted_iota(jnp.int32, (CHUNK, HEAD), 1)
        rows = pl.ds(pl.multiple_of(i * CHUNK, CHUNK), CHUNK)
        hot[rows, :] = jnp.where(block + i * 8 == lane, 1.0, 0.0).astype(jnp.bfloat16)
        return 0

    lax.fori_loop(0, 16, fill_hot, 0)
    for block in range(8):
        mine = order_smem[group * 8 + block]
        for half in range(2):
            order = jnp.broadcast_to(order_ref[:, half * HEAD:(half + 1) * HEAD], (32, HEAD))
            bias = jnp.where(order >= mine, MASKED, 0.0).astype(jnp.bfloat16)
            for h in range(4):
                qa[half, pl.ds(block // 2 * 256 + h * 64 + block % 2 * 32, 32), HEAD:] = bias

    for copy in own[:2]:
        copy.wait()
    for copy in exchanged:
        copy.wait_recv()

    def sibling_copy(layer, g, i):
        return remote(kv.at[layer, g], kv.at[layer, g], sib_send.at[i], sib_recv.at[i],
                      (1 - section, ctx))

    class Rings:
        def __init__(self, na, nb, z_first):
            self.na, self.nb, self.z_first = na, nb, z_first
            self.events = ring_events(na, nb)
            self.index = {e: i for i, e in enumerate(self.events)}

        def chunk(self, a, b):
            y_from, z_from = (y - b, z - a) if self.z_first else (y - a, z - b)
            return lax.rem(y_from + NY, NY) * NZ + lax.rem(z_from + NZ, NZ)

        def copy(self, g, event, half, da=0, db=1):
            slot = (self.index[event], 1 if half == 1 else 0)
            piece = kv.at[section, g] if half is None else kv.at[section, g, pl.ds(2 * half, 2)]
            device = at(y + db, z + da) if self.z_first else at(y + da, z + db)
            return remote(piece, piece, ring_send.at[slot], ring_recv.at[slot], device)

        def onward(self, event):
            a, b = event
            far_a, far_b = self.na // 2, self.nb // 2
            passed = []
            for sign in (1, -1):
                if b == 0 and a != far_a and a * sign >= 0:
                    to = a + sign
                    if abs(to) == far_a:
                        passed.append(((far_a, 0), 0 if sign > 0 else 1, sign, 0))
                    else:
                        passed.append(((to, 0), None, sign, 0))
            for sign in (1, -1):
                if b != far_b and b * sign >= 0:
                    to = b + sign
                    if abs(to) == far_b:
                        passed.append(((a, far_b), 0 if sign > 0 else 1, 0, sign))
                    else:
                        passed.append(((a, to), None, 0, sign))
            return passed

        def handle(self, i):
            a, b = event = self.events[i]
            g = self.chunk(a, b)
            if i:
                split = b == self.nb // 2 or (b == 0 and a == self.na // 2)
                for half in (0, 1) if split else (None,):
                    self.copy(g, event, half).wait_recv()
            sibling_copy(section, g, i).start()
            for to, half, da, db in self.onward(event):
                self.copy(g, to, half, da, db).start()

        def finish(self):
            for i, event in enumerate(self.events):
                g = self.chunk(*event)
                for to, half, da, db in self.onward(event):
                    self.copy(g, to, half, da, db).wait_send()
                sibling_copy(section, g, i).wait_send()

    first, second = Rings(NZ, NY, True), Rings(NY, NZ, False)

    def advance(indices):
        @pl.when(section == 0)
        def _():
            for i in indices:
                first.handle(i)

        @pl.when(section == 1)
        def _():
            for i in indices:
                second.handle(i)
            for i in indices:
                sibling_copy(0, first.chunk(*first.events[i]), i).wait_recv()

    def arrived(j):
        packed = [[(e[0] + 8) * 16 + e[1] + 8 for e in first.events[c::4]] for c in range(4)]
        places = [jnp.int32(row[0]) for row in packed]
        for n in range(1, 8):
            now = j == n
            places = [jnp.where(now, row[n], place) for row, place in zip(packed, places)]
        return [first.chunk(place // 16 - 8, place % 16 - 8) for place in places]

    advance([0])
    advance([1, 2, 3, 4])
    own[2].wait()
    wait_queries(0)
    for copy in exchanged:
        copy.wait_send()

    def widen(v):
        return jnp.concatenate([v, jnp.ones(v.shape, jnp.bfloat16)], axis=1)

    def product(q, k):
        return lax.dot_general(q, k, (((1,), (1,)), ((), ())), preferred_element_type=jnp.float32)

    def begin(layer):
        for xs in range(NX):
            rows = pl.ds(xs * ROW_TILE, ROW_TILE)
            q = qx[layer, xs]
            if layer == 1:
                gain = gain_ref[:, pl.ds(pl.multiple_of(x * 1024 + section * 512, 512), 512)]
                q = (q.astype(jnp.float32)
                     + gain * o_s[0, xs].astype(jnp.float32)).astype(jnp.bfloat16)
            q = jnp.concatenate([q[:, h * HEAD:(h + 1) * HEAD] for h in range(4)], axis=0)
            for half in range(2):
                qa[half, rows, :HEAD] = q
            pair = pl.ds(xs // 2 * 2, 2)
            own_k = kv[layer, group, pair, 0].reshape(CHUNK // 2, HEAD)
            own_v = widen(kv[layer, group, pair, 1].reshape(CHUNK // 2, HEAD))
            s = product(q, own_k)
            r = lax.broadcasted_iota(jnp.int32, s.shape, 0)
            t = lax.broadcasted_iota(jnp.int32, s.shape, 1)
            seen = (t // 32 == xs % 2 * 2 + (r % 64) // 32) & (t % 32 <= r % 32)
            s = jnp.where(seen, s, MASKED)
            m = jnp.max(s, axis=1, keepdims=True)
            p = jnp.exp2((s - m) * LOG2_SCALE).astype(jnp.bfloat16)
            acc_s[rows, :] = jnp.dot(p, own_v, preferred_element_type=jnp.float32)
            m_s[rows, :] = jnp.broadcast_to(m, (ROW_TILE, HEAD))

    def fold(layer, chunk_groups, tiles):
        operands = []
        for chunks in chunk_groups:
            keys, values = [], []
            for g in chunks:
                k = kv[layer, g, :, 0].reshape(CHUNK, HEAD)
                rows = pl.ds(pl.multiple_of(lax.rem(g, 16) * CHUNK, CHUNK), CHUNK)
                keys.append(jnp.concatenate([k, hot[rows, :]], axis=1))
                values.append(kv[layer, g, :, 1].reshape(CHUNK, HEAD))
            operands.append((chunks, keys, widen(jnp.concatenate(values, axis=0))))
        items = [(operand, pl.ds(xs * ROW_TILE, ROW_TILE)) for operand in operands for xs in tiles]

        def scores(item):
            (chunks, keys, _), rows = item
            return jnp.concatenate(
                [product(qa[g // 16, rows, :], k) for g, k in zip(chunks, keys)], axis=1)

        def update(item, s):
            (_, _, v), rows = item
            m_old = m_s[rows, :]
            m_new = jnp.maximum(m_old, jnp.max(s, axis=1, keepdims=True))
            a = jnp.exp2((m_old - m_new) * LOG2_SCALE)
            wide = jnp.concatenate([m_new] * (s.shape[1] // HEAD), axis=1)
            p = jnp.exp2((s - wide) * LOG2_SCALE).astype(jnp.bfloat16)
            acc_s[rows, :] = (acc_s[rows, :] * jnp.concatenate([a, a], axis=1)
                              + jnp.dot(p, v, preferred_element_type=jnp.float32))
            m_s[rows, :] = m_new

        s = scores(items[0])
        for i, item in enumerate(items):
            later = scores(items[i + 1]) if i + 1 < len(items) else None
            update(item, s)
            s = later

    back = pl.ds(pl.multiple_of(x * 1024 + section * 512, 512), 512)

    def return_copy(layer, x_to):
        k = lax.rem(x_to + NX - x, NX)
        return remote(o_s.at[layer, x_to], out_ref.at[0, :, back], out_send.at[layer, x_to],
                      out_recv.at[section, k], (layer, group * NX + x_to))

    def own_return():
        return pltpu.make_async_copy(o_s.at[section, x], out_ref.at[0, :, back], out_own)

    def end(layer, tiles):
        for xs in tiles:
            rows = pl.ds(xs * ROW_TILE, ROW_TILE)
            out = (acc_s[rows, :HEAD] / acc_s[rows, HEAD:]).astype(jnp.bfloat16)
            o_s[layer, xs] = jnp.concatenate([out[h * 64:(h + 1) * 64] for h in range(4)], axis=1)

    def send_back(layer, tiles):
        for x_to in tiles:
            stays = (section == layer) & (x == x_to)

            @pl.when(jnp.logical_not(stays))
            def _():
                return_copy(layer, x_to).start()

            @pl.when(stays)
            def _():
                own_return().start()

    begin(0)

    def step0(j, _):
        chunks = arrived(j)
        for half in range(2):
            fold(0, [chunks], (2 * half, 2 * half + 1))
            for i in range(7):
                @pl.when(j == i)
                def _():
                    advance([e for e in (4 * i + 4 + 2 * half, 4 * i + 5 + 2 * half) if e > 4])

        @pl.when((j == 1) & (section == 1))
        def _():
            send_queries(1)

        return 0

    lax.fori_loop(0, 8, step0, 0)
    end(0, range(NX))

    @pl.when(section == 0)
    def _():
        for i, event in enumerate(second.events):
            sibling_copy(1, second.chunk(*event), i).wait_recv()

    wait_queries(1)
    begin(1)
    send_back(0, range(NX))

    for tiles in ((0, 1), (2, 3)):
        def step1(j, _):
            fold(1, [[8 * j + 4 * i + c for c in range(4)] for i in range(2)], tiles)
            return 0

        lax.fori_loop(0, 4, step1, 0)
        end(1, tiles)
        send_back(1, tiles)

    @pl.when(section == 0)
    def _():
        first.finish()

    @pl.when(section == 1)
    def _():
        second.finish()

    for core in range(2):
        for k in range(1, NX):
            query_copy(core, k).wait_send()
    query_copy(1 - section, 0).wait_send()
    own_return().wait()
    for layer in range(2):
        for x_to in range(NX):
            @pl.when(jnp.logical_not((section == layer) & (x == x_to)))
            def _():
                return_copy(layer, x_to).wait_send()
    for core in range(2):
        for k in range(1, NX):
            remote(o_s.at[0, 0], out_ref.at[0, :, back], out_send.at[core, k],
                   out_recv.at[core, k], (1 - section, ctx)).wait_recv()

        @pl.when(section != core)
        def _():
            remote(o_s.at[0, 0], out_ref.at[0, :, back], out_send.at[core, 0],
                   out_recv.at[core, 0], (1 - section, ctx)).wait_recv()


def body(queries, key_rows, rows_of_value, query_gain, block_order):
    rows = queries.shape[1]
    dma = pltpu.SemaphoreType.DMA
    hbm = pl.BlockSpec(memory_space=pl.ANY)
    vmem = pl.BlockSpec(memory_space=pltpu.VMEM)
    return pl.pallas_call(
        layer_kernel,
        out_shape=jax.ShapeDtypeStruct(queries.shape, jnp.bfloat16),
        in_specs=[hbm, hbm, hbm, vmem, vmem, pl.BlockSpec(memory_space=pltpu.SMEM)],
        out_specs=hbm,
        scratch_shapes=[
            pltpu.VMEM((2, GROUPS, NX, 2, rows, HEAD), jnp.bfloat16),
            pltpu.VMEM((2, NX, rows, 4 * HEAD), jnp.bfloat16),
            pltpu.VMEM((4096, HEAD), jnp.bfloat16),
            pltpu.VMEM((2, 1024, 2 * HEAD), jnp.bfloat16),
            pltpu.VMEM((1024, HEAD), jnp.float32),
            pltpu.VMEM((1024, 2 * HEAD), jnp.float32),
            pltpu.VMEM((2, NX, rows, 4 * HEAD), jnp.bfloat16),
            dma((2, 4)), dma((2, 4)), dma((3, 2)), dma((3, 2)), dma((32, 2)), dma((32, 2)),
            dma((32,)), dma((32,)), dma((3,)), dma((2, 4)), dma((2, 4)), dma,
        ],
        compiler_params=pltpu.CompilerParams(
            collective_id=0, has_side_effects=True, vmem_limit_bytes=60 * 2**20),
    )(queries, key_rows, rows_of_value, query_gain[None, :], block_order[None, :], block_order)


def solution(mesh):
    placed = (
        P("section", "ctx", None),
        P("section", "ctx", None),
        P("section", "ctx", None),
        P(),
        P(),
    )
    return jax.shard_map(
        body, mesh=mesh, in_specs=placed, out_specs=P("section", "ctx", None), check_vma=False
    )
```
